32 devices in a mesh: rep: 2 (over y), slab: 16 (over z, x, core).
Axes of the slice: x: 2, y: 2, z: 4, core: 2. Of those that a mesh axis runs over, the one named last changes fastest.
Arguments:
- spins: float32 [8, 3, 128, 16, 256], P('rep', None, 'slab'), as said below
- couplings: int32 [3, 128, 16, 256], P(None, 'slab'), may hold values from 0 to 1
- source: int32 [8], replicated, may hold values from 0 to 7, as said below
Outputs:
- annealed: float32 [8, 3, 128, 16, 256], P('rep', None, 'slab')
The draws below stay inside these ranges and needn't reach their ends.
Inputs may be any that keep to these rules, and one draw needn't show every extreme that they name: Slot d = g * 4 + l (rep group g, local index l) either copies its own replica (source[d] = d) or copies a replica of group (g + 1 + l // 2) mod 2 whose own slot copies itself. In every group at least one of slots 0 and 1 and at least one of slots 2 and 3 copy in this way. Some group has two slots that copy replicas of one other group. `spins`: each replica is a unit vector at every site.
All inputs are finite; a program needn't handle non-finite values.
Results may differ from the reference program's by a relative error of at most 0.0003.
Values sent between devices are 32-bit elements; how exact they have to be, the bound alone decides.
A program may use at most 64 MiB of HBM per device.

```python
import jax
import jax.numpy as jnp
from jax import lax

NX = 256
NY = 16
REP_DEV = 4
SWEEPS = 4
NZ = 128
REPLICAS = 8
N_REP = 2


def draw_spins(key, part):
    raw = jax.random.normal(key, (REPLICAS, 3, NZ, NY, NX), jnp.float32)
    length = jnp.sqrt(jnp.sum(raw * raw, axis=1, keepdims=True))
    return raw / jnp.maximum(length, 0.001)


def draw_source(key, part):
    key_keep, key_group, key_bits, key_pick, key_low = jax.random.split(jax.random.fold_in(key, 7), 5)
    groups = jnp.arange(N_REP, dtype=jnp.int32)
    local = jnp.arange(REP_DEV, dtype=jnp.int32)
    keep_slot = 2 + jax.random.randint(key_keep, (N_REP,), 0, REP_DEV - 2)
    low_slot = jax.random.randint(key_low, (N_REP,), 0, 2)
    first_group = jax.random.randint(key_group, (), 0, N_REP)
    bits = jax.random.randint(key_bits, (N_REP, REP_DEV), 0, 2)
    forced = (groups[:, None] == first_group) & (local[None, :] < 2)
    forced = forced | (local[None, :] == low_slot[:, None]) | (local[None, :] == (5 - keep_slot)[:, None])
    survive = local[None, :] == keep_slot[:, None]
    killed = ((bits == 1) | forced) & jnp.logical_not(survive)
    scores = jax.random.randint(key_pick, (N_REP, REP_DEV), 0, 1 << 20) * REP_DEV + local[None, :]
    masked = jnp.where(killed, -1, scores)
    picked = jnp.argmax(masked, axis=1).astype(jnp.int32)
    giver = (groups[:, None] + 1 + local[None, :] // 2) % N_REP
    anchor = giver * REP_DEV + jnp.take(picked, giver)
    own = groups[:, None] * REP_DEV + local[None, :]
    return jnp.where(killed, anchor, own).reshape(-1).astype(jnp.int32)


def touch_ends(drawn, key, smallest, largest):
    dims = drawn.shape
    place = [jax.random.randint(jax.random.fold_in(key, axis), (), 0, dims[axis]) for axis in range(len(dims))]
    drawn = drawn.at[tuple(place)].set(smallest)
    longest = dims.index(max(dims))
    place[longest] = (place[longest] + 1) % dims[longest]
    return drawn.at[tuple(place)].set(largest)


def setup_inputs(seed: int = 0) -> dict:
    arg_keys = jax.random.split(jax.random.key(seed), 4)
    spins = draw_spins(jax.random.fold_in(arg_keys[3], 71), 0)
    couplings = touch_ends(jax.random.randint(arg_keys[1], (3, NZ, NY, NX), 0, 2), jax.random.fold_in(arg_keys[1], 1), 0, 1).astype(jnp.int32)
    source = draw_source(jax.random.fold_in(arg_keys[3], 71), 0)
    return dict(spins=spins, couplings=couplings, source=source)


def field_ref(lattice, bonds):
    east = bonds[0] * jnp.roll(lattice, -1, axis=3)
    west = jnp.roll(bonds[0] * lattice, 1, axis=3)
    north = bonds[1] * jnp.roll(lattice, -1, axis=2)
    south = jnp.roll(bonds[1] * lattice, 1, axis=2)
    upper = bonds[2] * jnp.roll(lattice, -1, axis=1)
    lower = jnp.roll(bonds[2] * lattice, 1, axis=1)
    return ((((east + west) + north) + south) + upper) + lower


def relax_ref(lattice, local_field, mask):
    along = jnp.sum(lattice * local_field, axis=0, keepdims=True)
    strength = jnp.sum(local_field * local_field, axis=0, keepdims=True)
    turned = 2.0 * along / jnp.maximum(strength, 1.0) * local_field - lattice
    return jnp.where(mask, turned, lattice)


def reference(spins, couplings, source):
    bonds = (2 * couplings - 1).astype(jnp.float32)
    copied = jnp.take(spins, source.astype(jnp.int32), axis=0)
    shape = (NZ, NY, NX)
    total = lax.broadcasted_iota(jnp.int32, shape, 0) + lax.broadcasted_iota(jnp.int32, shape, 1) + lax.broadcasted_iota(jnp.int32, shape, 2)
    masks = [((total % 2) == colour)[None] for colour in range(2)]

    def one_replica(lattice):
        for sweep in range(SWEEPS):
            for colour in range(2):
                local_field = field_ref(lattice, bonds)
                lattice = relax_ref(lattice, local_field, masks[colour])
        return lattice

    return lax.map(one_replica, copied)
```

```python
import functools

import jax
import jax.numpy as jnp
from jax import lax
from jax.experimental import pallas as pl
from jax.experimental.pallas import tpu as pltpu
from jax.sharding import PartitionSpec as P

SWEEPS = 4
GROUP = 5
WIDTH = 2
MESH = pl.DeviceIdType.MESH


def reverse_rows(value, row):
    count = value.shape[0]
    shift = 1
    while shift < count:
        down = pltpu.roll(value, shift, 0)
        if 2 * shift == count:
            value = down
        else:
            value = jnp.where((row & shift) == 0, pltpu.roll(value, count - shift, 0), down)
        shift *= 2
    return value


def halo_items(width, colour, first):
    below = [(0, 1 - colour)] + [(d, c) for d in range(1, width) for c in range(2)]
    above = [(d, c) for d in range(width - 1) for c in range(2)] + [(width - 1, 1 - colour)]
    if not first and width % 2 == 0:
        below.remove((width - 1, 0))
        above.remove((0, 0))
    return below, above


def kernel(n_rep, n_slab, source, spins_hbm, coup_hbm, out, spins, coup, raw, work, bonds, low, high, stage, land, res, c_send, c_recv, h_send, h_recv, r_send, r_recv, in_sem):
    rep_dev, comps, planes, rows, cols = spins.shape
    pairs = rep_dev // 2
    width, half = WIDTH, rows // 2
    exchanges = 2 * SWEEPS // width
    group, slab = lax.axis_index("rep"), lax.axis_index("slab")
    up, down = lax.rem(slab + 1, n_slab), lax.rem(slab + n_slab - 1, n_slab)
    offsets = [(1 + j) % n_rep for j in range(pairs)]
    remote = [j for j in range(pairs) if offsets[j]]

    loads = [pltpu.make_async_copy(spins_hbm.at[pl.ds(2 * r, 2)], spins.at[pl.ds(2 * r, 2)], in_sem.at[r]) for r in range(pairs)]
    loads.append(pltpu.make_async_copy(coup_hbm, coup, in_sem.at[pairs]))
    for copy in loads:
        copy.start()

    barrier = pltpu.get_barrier_semaphore()
    for side in (up, down):
        pl.semaphore_signal(barrier, inc=1, device_id=(group, side), device_id_type=MESH)
    for j in remote:
        giver = lax.rem(group + offsets[j], n_rep)
        pl.semaphore_signal(barrier, inc=1, device_id=(giver, slab), device_id_type=MESH)
    def remote_copy(src, dst, send, recv, device):
        copy = pltpu.make_async_remote_copy(
            src_ref=src, dst_ref=dst, send_sem=send, recv_sem=recv, device_id=device, device_id_type=MESH
        )
        copy.start()
        return copy

    row = lax.broadcasted_iota(jnp.int32, (half, cols), 0)
    site = row + lax.broadcasted_iota(jnp.int32, (half, cols), 1)

    def front(plane):
        return ((site + (slab * planes + plane + width)) & 1) == 0

    def pack(mask, first, second):
        second = reverse_rows(second, row)
        return jnp.where(mask, first, second), jnp.where(mask, second, first)

    copies = {}

    def send_halo(r, e):
        colour = (e * width) % 2
        below, above = halo_items(width, colour, e == 0)
        for side, (items, start, device) in enumerate(((below, planes, up), (above, width, down))):
            for i, (d, c) in enumerate(items):
                for k in range(comps):
                    stage[e, side, r, i, k] = work[r, start + d, c, k]
            copies[r, e, side] = remote_copy(
                stage.at[e, side, r, pl.ds(0, len(items))],
                land.at[e, side, r, pl.ds(0, len(items))], h_send.at[e, side, r],
                h_recv.at[e, side, r],
                (group, device),
            )

    def take_halo(r, e):
        colour = (e * width) % 2
        below, above = halo_items(width, colour, e == 0)
        for side, (items, start) in enumerate(((below, 0), (above, planes + width))):
            copies[r, e, side].wait()
            for i, (d, c) in enumerate(items):
                for k in range(comps):
                    work[r, start + d, c, k] = land[e, side, r, i, k]

    kept = []
    for slot in range(rep_dev):
        own = group * rep_dev + slot
        kept.append(source[own] == own)

    for r in range(pairs):
        loads[r].wait()

        def pack_plane(p, carry, r=r):
            mask = front(p + width)
            for k in range(comps):
                value = jnp.where(kept[2 * r], spins[2 * r, k, p], spins[2 * r + 1, k, p])
                zero, one = pack(mask, value[:half], value[half:])
                work[r, p + width, 0, k] = zero
                work[r, p + width, 1, k] = one
                if r == 0 and remote:
                    raw[p, 0, k] = zero
                    raw[p, 1, k] = one
            return carry

        lax.fori_loop(0, planes, pack_plane, 0)

    def bonds_of(plane, jx, jy, jz, jz_below):
        mask = front(plane)
        jx, jy, jz, jz_below = [(2 * j - 1).astype(jnp.float32) for j in (jx, jy, jz, jz_below)]
        jw = pltpu.roll(jx, 1, 1)
        first, second = jy[:half], jy[half:]
        south_first = jnp.where(row == 0, second[half - 1 :], pltpu.roll(first, 1, 0))
        south_second = jnp.where(row == 0, first[half - 1 :], pltpu.roll(second, 1, 0))
        first_r = reverse_rows(second, row)
        south_r = reverse_rows(south_second, row)
        east = pack(mask, jx[:half], jx[half:])
        west = pack(mask, jw[:half], jw[half:])
        upper = pack(mask, jz[:half], jz[half:])
        lower = pack(mask, jz_below[:half], jz_below[half:])
        after = (jnp.where(mask, first, south_r), jnp.where(mask, south_r, first))
        before = (jnp.where(mask, south_first, first_r), jnp.where(mask, first_r, south_first))
        for i, bond in enumerate((east, west, after, before, upper, lower)):
            for c in range(2):
                bonds[plane, c, i] = bond[c]

    def own_bonds(p, carry):
        bonds_of(p + width, coup[0, p], coup[1, p], coup[2, p], coup[2, p - 1])
        return carry

    loads[pairs].wait()
    lax.fori_loop(1, planes, own_bonds, 0)
    pl.semaphore_wait(barrier, 2 + len(remote))

    bond_copies = [remote_copy(coup.at[2, planes - width], low.at[2, 0], c_send.at[0], c_recv.at[0], (group, up))]
    if width > 1:
        bond_copies.append(
            remote_copy(coup.at[:, planes - width + 1 : planes], low.at[:, 1:width], c_send.at[1], c_recv.at[1], (group, up))
        )
        bond_copies.append(remote_copy(coup.at[:, 0 : width - 1], high, c_send.at[2], c_recv.at[2], (group, down)))
    inner = pl.ds(width, planes)
    results, late = [], []
    for n, j in enumerate(remote):
        taker = lax.rem(group + n_rep - offsets[j], n_rep)
        late.append(remote_copy(raw, work.at[pairs + n, inner], r_send.at[n, 0], r_recv.at[n, 0], (taker, slab)))
    for r in range(pairs - 1, -1, -1):
        send_halo(r, 0)
    for copy in bond_copies:
        copy.wait()
    for p in range(1, width):
        bonds_of(p, low[0, p], low[1, p], low[2, p], low[2, p - 1])
    bonds_of(width, coup[0, 0], coup[1, 0], coup[2, 0], low[2, width - 1])
    for p in range(width - 1):
        beneath = coup[2, planes - 1] if p == 0 else high[2, p - 1]
        bonds_of(planes + width + p, high[0, p], high[1, p], high[2, p], beneath)

    def half_sweep(r, colour, first, last):
        other = 1 - colour

        def turned(p):
            east, west, after, before, upper, lower = [bonds[p, colour, i] for i in range(6)]
            field, spin = [], []
            for k in range(comps):
                q = work[r, p, other, k]
                north = jnp.where(row == half - 1, q, pltpu.roll(q, half - 1, 0))
                south = jnp.where(row == 0, q, pltpu.roll(q, 1, 0))
                h = east * pltpu.roll(q, cols - 1, 1) + west * pltpu.roll(q, 1, 1)
                h = h + after * north + before * south
                h = h + upper * work[r, p + 1, other, k] + lower * work[r, p - 1, other, k]
                field.append(h)
                spin.append(work[r, p, colour, k])
            along = sum(s * h for s, h in zip(spin, field))
            strength = sum(h * h for h in field)
            scale = 2.0 * along / jnp.maximum(strength, 1.0)
            return [scale * h - s for s, h in zip(spin, field)]

        count = last - first
        step = max(g for g in range(1, GROUP + 1) if count % g == 0)

        def some_planes(i, carry):
            base = first + i * step
            new = [turned(base + n) for n in range(step)]
            for n in range(step):
                for k in range(comps):
                    work[r, base + n, colour, k] = new[n][k]
            return carry

        lax.fori_loop(0, count // step, some_planes, 0)

    def advance(r, e):
        take_halo(r, e)
        for i in range(width):
            half_sweep(r, (e * width + i) % 2, i + 1, planes + 2 * width - 1 - i)
        if e < exchanges - 1:
            send_halo(r, e + 1)
        elif 1 <= r < pairs:
            for n, j in enumerate(remote):
                taker = lax.rem(group + n_rep - offsets[j], n_rep)
                results.append(
                    remote_copy(work.at[r, inner], res.at[n, r - 1], r_send.at[n, r], r_recv.at[n, r], (taker, slab))
                )

    for e in range(exchanges):
        for r in range(pairs - 1, -1, -1):
            advance(r, e)
        if e == 0:
            for n, copy in enumerate(late):
                copy.wait_recv()
                send_halo(pairs + n, 0)
        elif e < exchanges - 1:
            for n in range(len(late)):
                advance(pairs + n, e - 1)

    def write(j):
        if j in remote:
            n = remote.index(j)
            given = lambda r, p, c, k: res[n, r - 1, p, c, k] if r else work[pairs + n, p + width, c, k]
        else:
            given = lambda r, p, c, k: work[r, p + width, c, k]

        def write_plane(p, carry):
            mask = front(p + width)
            for slot in (2 * j, 2 * j + 1):
                pair = lax.rem(source[group * rep_dev + slot], rep_dev) // 2
                for k in range(comps):
                    colours = []
                    for c in range(2):
                        value = given(0, p, c, k)
                        for r in range(1, pairs):
                            value = jnp.where(pair == r, given(r, p, c, k), value)
                        colours.append(jnp.where(kept[slot], work[j, p + width, c, k], value))
                    zero, one = colours
                    out[slot, k, p, :half] = jnp.where(mask, zero, one)
                    out[slot, k, p, half:] = reverse_rows(jnp.where(mask, one, zero), row)
            return carry

        lax.fori_loop(0, planes, write_plane, 0)

    def store(j):
        write(j)

    for j in range(pairs):
        if j not in remote:
            store(j)
    for e in range(max(exchanges - 2, 0), exchanges):
        for n in range(len(late)):
            advance(pairs + n, e)
    for copy in late:
        copy.wait_send()
    for copy in results:
        copy.wait()
    for j in remote:
        store(j)


def solution(mesh):
    n_rep, n_slab = mesh.shape["rep"], mesh.shape["slab"]

    def local(spins, couplings, source):
        rep_dev, comps, planes, rows, cols = spins.shape
        pairs, half, width = rep_dev // 2, rows // 2, WIDTH
        exchanges, items = 2 * SWEEPS // width, 2 * width - 1
        n_remote = sum(1 for j in range(pairs) if (1 + j) % n_rep)
        deep = planes + 2 * width
        f32, i32, dma = jnp.float32, jnp.int32, pltpu.SemaphoreType.DMA
        annealed = pl.pallas_call(
            functools.partial(kernel, n_rep, n_slab),
            out_shape=pltpu.VMEM(spins.shape, f32),
            in_specs=[
                pl.BlockSpec(memory_space=pltpu.SMEM),
                pl.BlockSpec(memory_space=pl.ANY),
                pl.BlockSpec(memory_space=pl.ANY),
            ],
            out_specs=pl.BlockSpec(memory_space=pltpu.VMEM),
            scratch_shapes=[
                pltpu.VMEM(spins.shape, f32),
                pltpu.VMEM(couplings.shape, i32),
                pltpu.VMEM((planes, 2, comps, half, cols), f32),
                pltpu.VMEM((pairs + n_remote, deep, 2, comps, half, cols), f32),
                pltpu.VMEM((deep, 2, 6, half, cols), f32),
                pltpu.VMEM((3, width, rows, cols), i32),
                pltpu.VMEM((3, max(width - 1, 1), rows, cols), i32),
                pltpu.VMEM((exchanges, 2, pairs + n_remote, items, comps, half, cols), f32),
                pltpu.VMEM((exchanges, 2, pairs + n_remote, items, comps, half, cols), f32),
                pltpu.VMEM((max(n_remote, 1), pairs - 1, planes, 2, comps, half, cols), f32),
                dma((3,)),
                dma((3,)),
                dma((exchanges, 2, pairs + n_remote)),
                dma((exchanges, 2, pairs + n_remote)),
                dma((max(n_remote, 1), pairs)),
                dma((max(n_remote, 1), pairs)),
                dma((pairs + 1,)),
            ],
            compiler_params=pltpu.CompilerParams(collective_id=0, has_side_effects=True),
        )(source, spins, couplings)
        return annealed

    in_specs = (P("rep", None, "slab", None, None), P(None, "slab", None, None), P())
    out_specs = P("rep", None, "slab", None, None)
    return jax.shard_map(local, mesh=mesh, in_specs=in_specs, out_specs=out_specs, check_vma=False)
```

```python
import functools

import jax
import jax.numpy as jnp
from jax import lax
from jax.experimental import pallas as pl
from jax.experimental.pallas import tpu as pltpu
from jax.sharding import PartitionSpec as P

SWEEPS = 4
GROUP = 5
WIDTH = 2
FAR = 4
MESH = pl.DeviceIdType.MESH


def reverse_rows(value, row):
    count = value.shape[0]
    shift = 1
    while shift < count:
        down = pltpu.roll(value, shift, 0)
        if 2 * shift == count:
            value = down
        else:
            value = jnp.where((row & shift) == 0, pltpu.roll(value, count - shift, 0), down)
        shift *= 2
    return value


def kernel(n_rep, n_slab, source, spins_hbm, coup_hbm, out, spins, coup, raw, work, bonds, low, high, low_far, high_far, res, land, land_far, stage, c_send, c_recv, h_send, h_recv, x_send, x_recv, r_send, r_recv, m_send, m_recv, in_sem):
    rep_dev, comps, planes, rows, cols = spins.shape
    pairs, half, rounds = rep_dev // 2, rows // 2, SWEEPS
    edge = work.shape[2] - planes >> 1
    depth = min(FAR, edge)
    group, slab = lax.axis_index("rep"), lax.axis_index("slab")
    up, down = lax.rem(slab + 1, n_slab), lax.rem(slab + n_slab - 1, n_slab)
    far = depth > WIDTH
    far_below, far_above = slab == 0, up == 0
    offsets = [(1 + j) % n_rep for j in range(pairs)]
    remote = [j for j in range(pairs) if offsets[j]]
    guests = [pairs + n for n in range(len(remote))]
    loads = [pltpu.make_async_copy(spins_hbm.at[pl.ds(2 * r, 2)], spins.at[pl.ds(2 * r, 2)], in_sem.at[r]) for r in range(pairs)]
    loads.append(pltpu.make_async_copy(coup_hbm, coup, in_sem.at[pairs]))
    for copy in loads:
        copy.start()

    barrier = pltpu.get_barrier_semaphore()
    for side in (up, down):
        pl.semaphore_signal(barrier, inc=1, device_id=(group, side), device_id_type=MESH)
    for j in remote:
        giver = lax.rem(group + offsets[j], n_rep)
        pl.semaphore_signal(barrier, inc=1, device_id=(giver, slab), device_id_type=MESH)

    row = lax.broadcasted_iota(jnp.int32, (half, cols), 0)
    site = row + lax.broadcasted_iota(jnp.int32, (half, cols), 1)

    def front(plane):
        return ((site + (slab * planes + plane + edge)) & 1) == 0

    def pack(mask, first, second):
        second = reverse_rows(second, row)
        return jnp.where(mask, first, second), jnp.where(mask, second, first)

    def remote_copy(src, dst, send, recv, device):
        return pltpu.make_async_remote_copy(
            src_ref=src, dst_ref=dst, send_sem=send, recv_sem=recv, device_id=device, device_id_type=MESH
        )

    def when(condition, action):
        if condition is None:
            action()
        else:
            pl.when(condition)(action)

    def halo_copies(r, e, side):
        start, near, device = ((edge + planes - WIDTH, edge + planes - 1, up), (edge, edge, down))[side]
        copies = [remote_copy(
            work.at[r, 1, pl.ds(start, WIDTH)], land.at[r, e, side, pl.ds(0, WIDTH)],
            h_send.at[r, e, side, 0], h_recv.at[r, e, side, 0], (group, device),
        )]
        if e == 0:
            copies.append(remote_copy(
                work.at[r, 0, near], land.at[r, e, side, WIDTH],
                h_send.at[r, e, side, 1], h_recv.at[r, e, side, 1], (group, device),
            ))
        return copies

    def skips(r, e):
        return far and e % 2 == 1

    def send_halo(r, e):
        for side in range(2):
            for copy in halo_copies(r, e, side):
                when(jnp.logical_not((far_above, far_below)[side]) if skips(r, e) else None, copy.start)

    def take_halo(r, e):
        for side in range(2):
            for copy in halo_copies(r, e, side):
                when(jnp.logical_not((far_above, far_below)[side]) if skips(r, e) else None, copy.wait_send)
        for side in range(2):
            def take(side=side):
                for copy in halo_copies(r, e, side):
                    copy.wait_recv()
                start, near = ((edge - WIDTH, edge - 1), (edge + planes, edge + planes))[side]
                for k in range(comps):
                    for d in range(WIDTH):
                        work[r, 1, start + d, k] = land[r, e, side, d, k]
                    if e == 0:
                        work[r, 0, near, k] = land[r, e, side, WIDTH, k]
            when(jnp.logical_not((far_below, far_above)[side]) if skips(r, e) else None, take)

    def far_starts(side):
        return ((planes - depth + 1, planes - depth), (1, WIDTH))[side]

    def far_copies(r, e, side):
        device = (up, down)[side]
        spare = depth - WIDTH
        return [
            remote_copy(
                stage.at[r, e // 2 - 1, side, c] if e else raw.at[r, c, pl.ds(far_starts(side)[c], spare)],
                land_far.at[r, e // 2, side, c], x_send.at[r, e // 2, side, c], x_recv.at[r, e // 2, side, c],
                (group, device),
            )
            for c in range(2)
        ]

    def send_far(r, e):
        for side in range(2):
            def send(side=side):
                if e:
                    for c in range(2):
                        for d in range(depth - WIDTH):
                            for k in range(comps):
                                stage[r, e // 2 - 1, side, c, d, k] = work[r, c, edge + far_starts(side)[c] + d, k]
                for copy in far_copies(r, e, side):
                    copy.start()
            pl.when((far_above, far_below)[side])(send)

    def take_far(r, e):
        for side in range(2):
            def sent(side=side):
                for copy in far_copies(r, e, side):
                    copy.wait_send()
            pl.when((far_above, far_below)[side])(sent)

            def take(side=side):
                starts = ((edge - depth + 1, edge - depth), (edge + planes + 1, edge + planes + WIDTH))[side]
                starts = (starts[0], starts[1])
                for copy in far_copies(r, e, side):
                    copy.wait_recv()
                for c in range(2):
                    for d in range(depth - WIDTH):
                        for k in range(comps):
                            work[r, c, starts[c] + d, k] = land_far[r, e // 2, side, c, d, k]
            pl.when((far_below, far_above)[side])(take)

    kept = []
    for slot in range(rep_dev):
        own = group * rep_dev + slot
        kept.append(source[own] == own)

    for r in range(pairs):
        loads[r].wait()

        def pack_plane(p, carry, r=r):
            mask = front(p + edge)
            for k in range(comps):
                value = jnp.where(kept[2 * r], spins[2 * r, k, p], spins[2 * r + 1, k, p])
                for c, part in enumerate(pack(mask, value[:half], value[half:])):
                    work[r, c, p + edge, k] = part
                    raw[r, c, p, k] = part
            return carry

        lax.fori_loop(0, planes, pack_plane, 0)

    def bonds_of(plane, jx, jy, jz, jz_below):
        mask = front(plane)
        jx, jy, jz, jz_below = [(2 * j - 1).astype(jnp.float32) for j in (jx, jy, jz, jz_below)]
        jw = pltpu.roll(jx, 1, 1)
        first, second = jy[:half], jy[half:]
        south_first = jnp.where(row == 0, second[half - 1 :], pltpu.roll(first, 1, 0))
        south_second = jnp.where(row == 0, first[half - 1 :], pltpu.roll(second, 1, 0))
        first_r = reverse_rows(second, row)
        south_r = reverse_rows(south_second, row)
        east = pack(mask, jx[:half], jx[half:])
        west = pack(mask, jw[:half], jw[half:])
        upper = pack(mask, jz[:half], jz[half:])
        lower = pack(mask, jz_below[:half], jz_below[half:])
        after = (jnp.where(mask, first, south_r), jnp.where(mask, south_r, first))
        before = (jnp.where(mask, south_first, first_r), jnp.where(mask, first_r, south_first))
        for i, bond in enumerate((east, west, after, before, upper, lower)):
            for c in range(2):
                bonds[plane, c, i] = bond[c]

    def own_bonds(p, carry):
        bonds_of(p + edge, coup[0, p], coup[1, p], coup[2, p], coup[2, p - 1])
        return carry

    loads[pairs].wait()
    pl.semaphore_wait(barrier, 2 + len(remote))

    spans = [(0, WIDTH), (planes - WIDTH, WIDTH), (WIDTH, planes - 2 * WIDTH)]

    def raw_copy(n, i):
        taker = lax.rem(group + n_rep - offsets[remote[n]], n_rep)
        span = pl.ds(*spans[i])
        return remote_copy(raw.at[0, :, span], raw.at[pairs + n, :, span], r_send.at[n, i], r_recv.at[n, i], (taker, slab))

    def result_copy(n, r, i):
        taker = lax.rem(group + n_rep - offsets[remote[n]], n_rep)
        start, count = spans[i]
        return remote_copy(
            work.at[r, :, pl.ds(start + edge, count)], res.at[n, r - 1, :, pl.ds(start, count)],
            m_send.at[n, r - 1, i], m_recv.at[n, r - 1, i], (taker, slab),
        )

    bond_copies = [
        remote_copy(coup.at[2, planes - WIDTH], low.at[2, 0], c_send.at[0], c_recv.at[0], (group, up)),
        remote_copy(coup.at[:, planes - 1], low.at[:, 1], c_send.at[1], c_recv.at[1], (group, up)),
        remote_copy(coup.at[:, 0], high, c_send.at[2], c_recv.at[2], (group, down)),
    ]
    far_bonds = []
    if far:
        far_bonds = [
            (0, remote_copy(coup.at[2, planes - depth], low_far.at[2, 0], c_send.at[3], c_recv.at[3], (group, up))),
            (0, remote_copy(coup.at[:, planes - depth + 1 : planes - 1], low_far.at[:, 1:], c_send.at[4], c_recv.at[4], (group, up))),
            (1, remote_copy(coup.at[:, 1 : depth - 1], high_far, c_send.at[5], c_recv.at[5], (group, down))),
        ]
    def take_far_bonds():
        for side, copy in far_bonds:
            pl.when((far_above, far_below)[side])(copy.wait_send)

        def below():
            for side, copy in far_bonds:
                if side == 0:
                    copy.wait_recv()

            def plane(i, carry):
                bonds_of(edge - depth + i, low_far[0, i], low_far[1, i], low_far[2, i], low_far[2, i - 1])
                return carry

            lax.fori_loop(1, depth - 1, plane, 0)

        def above():
            for side, copy in far_bonds:
                if side == 1:
                    copy.wait_recv()
            bonds_of(edge + planes + 1, high_far[0, 0], high_far[1, 0], high_far[2, 0], high[2])

            def plane(i, carry):
                bonds_of(edge + planes + 1 + i, high_far[0, i], high_far[1, i], high_far[2, i], high_far[2, i - 1])
                return carry

            lax.fori_loop(1, depth - 2, plane, 0)

        pl.when(far_below)(below)
        pl.when(far_above)(above)

    def half_sweep(r, colour, parts):
        other = 1 - colour

        def turned(p):
            east, west, after, before, upper, lower = [bonds[p, colour, i] for i in range(6)]
            field, spin = [], []
            for k in range(comps):
                q = work[r, other, p, k]
                north = jnp.where(row == half - 1, q, pltpu.roll(q, half - 1, 0))
                south = jnp.where(row == 0, q, pltpu.roll(q, 1, 0))
                h = east * pltpu.roll(q, cols - 1, 1) + west * pltpu.roll(q, 1, 1)
                h = h + after * north + before * south
                h = h + upper * work[r, other, p + 1, k] + lower * work[r, other, p - 1, k]
                field.append(h)
                spin.append(work[r, colour, p, k])
            along = sum(s * h for s, h in zip(spin, field))
            strength = sum(h * h for h in field)
            scale = 2.0 * along / jnp.maximum(strength, 1.0)
            return [scale * h - s for s, h in zip(spin, field)]

        planes_of = list(parts)
        new = [turned(p) for p in planes_of]
        for p, value in zip(planes_of, new):
            for k in range(comps):
                work[r, colour, p, k] = value[k]

    low_edge, top = edge, edge + planes - 1

    def sweep_range(r, colour, first, last):
        count = last - first
        step = max(g for g in range(1, GROUP + 1) if count % g == 0)

        def some_planes(i, carry):
            half_sweep(r, colour, [first + i * step + n for n in range(step)])
            return carry

        lax.fori_loop(0, count // step, some_planes, 0)

    def inner(r):
        sweep_range(r, 0, low_edge + 1, top)
        sweep_range(r, 1, low_edge + 2, top - 1)

    def outer(r):
        half_sweep(r, 0, [low_edge - 1, low_edge, top, top + 1])
        half_sweep(r, 1, [low_edge, low_edge + 1, top - 1, top])

    def advance(r, e):
        if skips(r, e):
            take_far(r, e - 1)
            for colour in range(2):
                pl.when(far_below)(functools.partial(half_sweep, r, colour, [low_edge - 3 + colour, low_edge - 2 + colour]))
                pl.when(far_above)(functools.partial(half_sweep, r, colour, [top + 2 - colour, top + 3 - colour]))
        take_halo(r, e)
        outer(r)
        if e < rounds - 1:
            send_halo(r, e + 1)
            if far and e % 2 == 1:
                send_far(r, e + 1)
        elif 1 <= r < pairs:
            for n in range(len(remote)):
                for i in range(2):
                    result_copy(n, r, i).start()

    def prepare(r, e):
        inner(r)
        if e == rounds - 1 and 1 <= r < pairs:
            for n in range(len(remote)):
                result_copy(n, r, 2).start()

    def settle(n, i):
        copy = raw_copy(n, i)
        copy.wait_recv()
        start, count = spans[i]

        def plane(p, carry):
            for c in range(2):
                for k in range(comps):
                    work[pairs + n, c, p + edge, k] = raw[pairs + n, c, p, k]
            return carry

        lax.fori_loop(start, start + count, plane, 0)

    for n in range(len(remote)):
        for i in range(2):
            raw_copy(n, i).start()
    for copy in bond_copies:
        copy.start()
    for r in range(pairs - 1, -1, -1):
        send_halo(r, 0)
    for n in range(len(remote)):
        raw_copy(n, 2).start()
    if far:
        for side, copy in far_bonds:
            pl.when((far_above, far_below)[side])(copy.start)
        for r in range(pairs - 1, -1, -1):
            send_far(r, 0)
    lax.fori_loop(1, planes, own_bonds, 0)
    for r in range(pairs - 1, -1, -1):
        inner(r)
    for copy in bond_copies:
        copy.wait()
    bonds_of(edge - 1, low[0, 1], low[1, 1], low[2, 1], low[2, 0])
    bonds_of(edge, coup[0, 0], coup[1, 0], coup[2, 0], low[2, 1])
    bonds_of(edge + planes, high[0], high[1], high[2], coup[2, planes - 1])

    own = list(range(pairs - 1, -1, -1))
    for i, r in enumerate(own):
        advance(r, 0)
        if i == 0:
            for n, g in enumerate(guests):
                settle(n, 0)
                settle(n, 1)
                send_halo(g, 0)
    for r in own:
        prepare(r, 1)
    if far:
        take_far_bonds()
    for r in own:
        advance(r, 1)
        prepare(r, 2)
    for n, g in enumerate(guests):
        settle(n, 2)
        if far:
            send_far(g, 0)
        inner(g)
        advance(g, 0)
        prepare(g, 1)
    for e in range(2, rounds):
        for r in own:
            advance(r, e)
            if e < rounds - 1:
                prepare(r, e + 1)
        for g in guests:
            advance(g, e - 1)
            prepare(g, e)

    def write(j):
        if j in remote:
            n = remote.index(j)
            given = lambda r, p, c, k: res[n, r - 1, c, p, k] if r else work[pairs + n, c, p + edge, k]
        else:
            given = lambda r, p, c, k: work[r, c, p + edge, k]

        def write_plane(p, carry):
            mask = front(p + edge)
            for slot in (2 * j, 2 * j + 1):
                pair = lax.rem(source[group * rep_dev + slot], rep_dev) // 2
                for k in range(comps):
                    colours = []
                    for c in range(2):
                        value = given(0, p, c, k)
                        for r in range(1, pairs):
                            value = jnp.where(pair == r, given(r, p, c, k), value)
                        colours.append(jnp.where(kept[slot], work[j, c, p + edge, k], value))
                    zero, one = colours
                    out[slot, k, p, :half] = jnp.where(mask, zero, one)
                    out[slot, k, p, half:] = reverse_rows(jnp.where(mask, one, zero), row)
            return carry

        lax.fori_loop(0, planes, write_plane, 0)

    for j in range(pairs):
        if j not in remote:
            write(j)
    for g in guests:
        advance(g, rounds - 1)
    for n in range(len(remote)):
        for i in range(3):
            raw_copy(n, i).wait_send()
            for r in range(1, pairs):
                result_copy(n, r, i).wait()
    for j in remote:
        write(j)


def solution(mesh):
    n_rep, n_slab = mesh.shape["rep"], mesh.shape["slab"]

    def local(spins, couplings, source):
        rep_dev, comps, planes, rows, cols = spins.shape
        pairs, half = rep_dev // 2, rows // 2
        n_remote = sum(1 for j in range(pairs) if (1 + j) % n_rep)
        depth = min(FAR, planes)
        spare = max(depth - WIDTH, 1)
        deep = planes + 2 * depth
        starts = pairs + n_remote
        f32, i32, dma = jnp.float32, jnp.int32, pltpu.SemaphoreType.DMA
        return pl.pallas_call(
            functools.partial(kernel, n_rep, n_slab),
            out_shape=pltpu.VMEM(spins.shape, f32),
            in_specs=[
                pl.BlockSpec(memory_space=pltpu.SMEM),
                pl.BlockSpec(memory_space=pl.ANY),
                pl.BlockSpec(memory_space=pl.ANY),
            ],
            out_specs=pl.BlockSpec(memory_space=pltpu.VMEM),
            scratch_shapes=[
                pltpu.VMEM(spins.shape, f32),
                pltpu.VMEM(couplings.shape, i32),
                pltpu.VMEM((starts, 2, planes, comps, half, cols), f32),
                pltpu.VMEM((starts, 2, deep, comps, half, cols), f32),
                pltpu.VMEM((deep, 2, 6, half, cols), f32),
                pltpu.VMEM((3, WIDTH, rows, cols), i32),
                pltpu.VMEM((3, rows, cols), i32),
                pltpu.VMEM((3, spare + 1, rows, cols), i32),
                pltpu.VMEM((3, spare, rows, cols), i32),
                pltpu.VMEM((max(n_remote, 1), pairs - 1, 2, planes, comps, half, cols), f32),
                pltpu.VMEM((starts, SWEEPS, 2, WIDTH + 1, comps, half, cols), f32),
                pltpu.VMEM((starts, (SWEEPS + 1) // 2, 2, 2, spare, comps, half, cols), f32),
                pltpu.VMEM((starts, max((SWEEPS - 1) // 2, 1), 2, 2, spare, comps, half, cols), f32),
                dma((6,)),
                dma((6,)),
                dma((starts, SWEEPS, 2, 2)),
                dma((starts, SWEEPS, 2, 2)),
                dma((starts, (SWEEPS + 1) // 2, 2, 2)),
                dma((starts, (SWEEPS + 1) // 2, 2, 2)),
                dma((max(n_remote, 1), 3)),
                dma((max(n_remote, 1), 3)),
                dma((max(n_remote, 1), pairs - 1, 3)),
                dma((max(n_remote, 1), pairs - 1, 3)),
                dma((pairs + 1,)),
            ],
            compiler_params=pltpu.CompilerParams(collective_id=0, has_side_effects=True),
        )(source, spins, couplings)

    in_specs = (P("rep", None, "slab", None, None), P(None, "slab", None, None), P())
    out_specs = P("rep", None, "slab", None, None)
    return jax.shard_map(local, mesh=mesh, in_specs=in_specs, out_specs=out_specs, check_vma=False)
```

```python
import functools

import jax
import jax.numpy as jnp
from jax import lax
from jax.experimental import pallas as pl
from jax.experimental.pallas import tpu as pltpu
from jax.sharding import PartitionSpec as P

SWEEPS = 4
GROUP = 5
WIDTH = 2
FAR = 4
MESH = pl.DeviceIdType.MESH


def reverse_rows(value, row):
    count = value.shape[0]
    shift = 1
    while shift < count:
        down = pltpu.roll(value, shift, 0)
        if 2 * shift == count:
            value = down
        else:
            value = jnp.where((row & shift) == 0, pltpu.roll(value, count - shift, 0), down)
        shift *= 2
    return value


def kernel(n_rep, n_slab, source, spins_hbm, coup_hbm, out, spins, coup, raw, work, bonds, low, high, low_far, high_far, res, land, land_far, stage, c_send, c_recv, h_send, h_recv, x_send, x_recv, r_send, r_recv, m_send, m_recv, in_sem):
    rep_dev, comps, planes, rows, cols = spins.shape
    pairs, half, rounds = rep_dev // 2, rows // 2, SWEEPS
    edge = work.shape[2] - planes >> 1
    depth = min(FAR, edge)
    group, slab = lax.axis_index("rep"), lax.axis_index("slab")
    up, down = lax.rem(slab + 1, n_slab), lax.rem(slab + n_slab - 1, n_slab)
    far = depth > WIDTH
    far_below, far_above = slab == 0, up == 0
    offsets = [(1 + j) % n_rep for j in range(pairs)]
    remote = [j for j in range(pairs) if offsets[j]]
    guests = [pairs + n for n in range(len(remote))]
    loads = [pltpu.make_async_copy(spins_hbm.at[pl.ds(2 * r, 2)], spins.at[pl.ds(2 * r, 2)], in_sem.at[r]) for r in range(pairs)]
    loads.append(pltpu.make_async_copy(coup_hbm, coup, in_sem.at[pairs]))
    for copy in loads:
        copy.start()

    barrier = pltpu.get_barrier_semaphore()
    for side in (up, down):
        pl.semaphore_signal(barrier, inc=1, device_id=(group, side), device_id_type=MESH)
    for j in remote:
        giver = lax.rem(group + offsets[j], n_rep)
        pl.semaphore_signal(barrier, inc=1, device_id=(giver, slab), device_id_type=MESH)

    row = lax.broadcasted_iota(jnp.int32, (half, cols), 0)
    site = row + lax.broadcasted_iota(jnp.int32, (half, cols), 1)

    def front(plane):
        return ((site + (slab * planes + plane + edge)) & 1) == 0

    def pack(mask, first, second):
        second = reverse_rows(second, row)
        return jnp.where(mask, first, second), jnp.where(mask, second, first)

    def remote_copy(src, dst, send, recv, device):
        return pltpu.make_async_remote_copy(
            src_ref=src, dst_ref=dst, send_sem=send, recv_sem=recv, device_id=device, device_id_type=MESH
        )

    def when(condition, action):
        if condition is None:
            action()
        else:
            pl.when(condition)(action)

    def halo_copies(r, e, side):
        start, near, device = ((edge + planes - WIDTH, edge + planes - 1, up), (edge, edge, down))[side]
        copies = [remote_copy(
            work.at[r, 1, pl.ds(start, WIDTH)], land.at[r, e, side, pl.ds(0, WIDTH)],
            h_send.at[r, e, side, 0], h_recv.at[r, e, side, 0], (group, device),
        )]
        if e == 0:
            copies.append(remote_copy(
                work.at[r, 0, near], land.at[r, e, side, WIDTH],
                h_send.at[r, e, side, 1], h_recv.at[r, e, side, 1], (group, device),
            ))
        return copies

    def skips(r, e):
        return far and r >= pairs and e % 2 == 1

    def send_halo(r, e):
        for side in range(2):
            for copy in halo_copies(r, e, side):
                when(jnp.logical_not((far_above, far_below)[side]) if skips(r, e) else None, copy.start)

    def take_halo(r, e):
        for side in range(2):
            for copy in halo_copies(r, e, side):
                when(jnp.logical_not((far_above, far_below)[side]) if skips(r, e) else None, copy.wait_send)
        for side in range(2):
            def take(side=side):
                for copy in halo_copies(r, e, side):
                    copy.wait_recv()
                start, near = ((edge - WIDTH, edge - 1), (edge + planes, edge + planes))[side]
                for k in range(comps):
                    for d in range(WIDTH):
                        work[r, 1, start + d, k] = land[r, e, side, d, k]
                    if e == 0:
                        work[r, 0, near, k] = land[r, e, side, WIDTH, k]
            when(jnp.logical_not((far_below, far_above)[side]) if skips(r, e) else None, take)

    def far_starts(side):
        return ((planes - depth + 1, planes - depth), (1, WIDTH))[side]

    def far_copies(r, e, side):
        device = (up, down)[side]
        spare = depth - WIDTH
        return [
            remote_copy(
                stage.at[r, e // 2 - 1, side, c] if e else raw.at[r, c, pl.ds(far_starts(side)[c], spare)],
                land_far.at[r, e // 2, side, c], x_send.at[r, e // 2, side, c], x_recv.at[r, e // 2, side, c],
                (group, device),
            )
            for c in range(2)
        ]

    def send_far(r, e):
        for side in range(2):
            def send(side=side):
                if e:
                    for c in range(2):
                        for d in range(depth - WIDTH):
                            for k in range(comps):
                                stage[r, e // 2 - 1, side, c, d, k] = work[r, c, edge + far_starts(side)[c] + d, k]
                for copy in far_copies(r, e, side):
                    copy.start()
            pl.when((far_above, far_below)[side])(send)

    def take_far(r, e):
        for side in range(2):
            def sent(side=side):
                for copy in far_copies(r, e, side):
                    copy.wait_send()
            pl.when((far_above, far_below)[side])(sent)

            def take(side=side):
                starts = ((edge - depth + 1, edge - depth), (edge + planes + 1, edge + planes + WIDTH))[side]
                for copy in far_copies(r, e, side):
                    copy.wait_recv()
                for c in range(2):
                    for d in range(depth - WIDTH):
                        for k in range(comps):
                            work[r, c, starts[c] + d, k] = land_far[r, e // 2, side, c, d, k]
            pl.when((far_below, far_above)[side])(take)

    kept = []
    for slot in range(rep_dev):
        own = group * rep_dev + slot
        kept.append(source[own] == own)

    for r in range(pairs):
        loads[r].wait()

        def pack_plane(p, carry, r=r):
            mask = front(p + edge)
            for k in range(comps):
                value = jnp.where(kept[2 * r], spins[2 * r, k, p], spins[2 * r + 1, k, p])
                for c, part in enumerate(pack(mask, value[:half], value[half:])):
                    work[r, c, p + edge, k] = part
                    raw[r, c, p, k] = part
            return carry

        lax.fori_loop(0, planes, pack_plane, 0)

    def bonds_of(plane, jx, jy, jz, jz_below):
        mask = front(plane)
        jx, jy, jz, jz_below = [(2 * j - 1).astype(jnp.float32) for j in (jx, jy, jz, jz_below)]
        jw = pltpu.roll(jx, 1, 1)
        first, second = jy[:half], jy[half:]
        south_first = jnp.where(row == 0, second[half - 1 :], pltpu.roll(first, 1, 0))
        south_second = jnp.where(row == 0, first[half - 1 :], pltpu.roll(second, 1, 0))
        first_r = reverse_rows(second, row)
        south_r = reverse_rows(south_second, row)
        east = pack(mask, jx[:half], jx[half:])
        west = pack(mask, jw[:half], jw[half:])
        upper = pack(mask, jz[:half], jz[half:])
        lower = pack(mask, jz_below[:half], jz_below[half:])
        after = (jnp.where(mask, first, south_r), jnp.where(mask, south_r, first))
        before = (jnp.where(mask, south_first, first_r), jnp.where(mask, first_r, south_first))
        for i, bond in enumerate((east, west, after, before, upper, lower)):
            for c in range(2):
                bonds[plane, c, i] = bond[c]

    def own_bonds(p, carry):
        bonds_of(p + edge, coup[0, p], coup[1, p], coup[2, p], coup[2, p - 1])
        return carry

    loads[pairs].wait()
    pl.semaphore_wait(barrier, 2 + len(remote))

    spans = [(0, WIDTH), (planes - WIDTH, WIDTH), (WIDTH, planes - 2 * WIDTH)]

    def raw_copy(n, i):
        taker = lax.rem(group + n_rep - offsets[remote[n]], n_rep)
        span = pl.ds(*spans[i])
        return remote_copy(raw.at[0, :, span], raw.at[pairs + n, :, span], r_send.at[n, i], r_recv.at[n, i], (taker, slab))

    early = [(0, 1, planes - 2), (1, WIDTH, planes - 2 * WIDTH)]
    pieces = early + [(0, 0, 1), (0, planes - 1, 1), (1, 0, WIDTH), (1, planes - WIDTH, WIDTH)]

    def result_copy(n, r, i):
        taker = lax.rem(group + n_rep - offsets[remote[n]], n_rep)
        c, start, count = pieces[i]
        return remote_copy(
            work.at[r, c, pl.ds(start + edge, count)], res.at[n, r - 1, c, pl.ds(start, count)],
            m_send.at[n, r - 1, i], m_recv.at[n, r - 1, i], (taker, slab),
        )

    bond_copies = [
        remote_copy(coup.at[2, planes - WIDTH], low.at[2, 0], c_send.at[0], c_recv.at[0], (group, up)),
        remote_copy(coup.at[:, planes - 1], low.at[:, 1], c_send.at[1], c_recv.at[1], (group, up)),
        remote_copy(coup.at[:, 0], high, c_send.at[2], c_recv.at[2], (group, down)),
    ]
    far_bonds = []
    if far:
        far_bonds = [
            (0, remote_copy(coup.at[2, planes - depth], low_far.at[2, 0], c_send.at[3], c_recv.at[3], (group, up))),
            (0, remote_copy(coup.at[:, planes - depth + 1 : planes - 1], low_far.at[:, 1:], c_send.at[4], c_recv.at[4], (group, up))),
            (1, remote_copy(coup.at[:, 1 : depth - 1], high_far, c_send.at[5], c_recv.at[5], (group, down))),
        ]
    def take_far_bonds():
        for side, copy in far_bonds:
            pl.when((far_above, far_below)[side])(copy.wait_send)

        def below():
            for side, copy in far_bonds:
                if side == 0:
                    copy.wait_recv()

            def plane(i, carry):
                bonds_of(edge - depth + i, low_far[0, i], low_far[1, i], low_far[2, i], low_far[2, i - 1])
                return carry

            lax.fori_loop(1, depth - 1, plane, 0)

        def above():
            for side, copy in far_bonds:
                if side == 1:
                    copy.wait_recv()
            bonds_of(edge + planes + 1, high_far[0, 0], high_far[1, 0], high_far[2, 0], high[2])

            def plane(i, carry):
                bonds_of(edge + planes + 1 + i, high_far[0, i], high_far[1, i], high_far[2, i], high_far[2, i - 1])
                return carry

            lax.fori_loop(1, depth - 2, plane, 0)

        pl.when(far_below)(below)
        pl.when(far_above)(above)

    def half_sweep(r, colour, parts):
        other = 1 - colour

        def turned(p):
            east, west, after, before, upper, lower = [bonds[p, colour, i] for i in range(6)]
            field, spin = [], []
            for k in range(comps):
                q = work[r, other, p, k]
                north = jnp.where(row == half - 1, q, pltpu.roll(q, half - 1, 0))
                south = jnp.where(row == 0, q, pltpu.roll(q, 1, 0))
                h = east * pltpu.roll(q, cols - 1, 1) + west * pltpu.roll(q, 1, 1)
                h = h + after * north + before * south
                h = h + upper * work[r, other, p + 1, k] + lower * work[r, other, p - 1, k]
                field.append(h)
                spin.append(work[r, colour, p, k])
            along = sum(s * h for s, h in zip(spin, field))
            strength = sum(h * h for h in field)
            scale = 2.0 * along / jnp.maximum(strength, 1.0)
            return [scale * h - s for s, h in zip(spin, field)]

        planes_of = list(parts)
        new = [turned(p) for p in planes_of]
        for p, value in zip(planes_of, new):
            for k in range(comps):
                work[r, colour, p, k] = value[k]

    low_edge, top = edge, edge + planes - 1

    def sweep_range(r, colour, first, last):
        count = last - first
        step = max(g for g in range(1, GROUP + 1) if count % g == 0)

        def some_planes(i, carry):
            half_sweep(r, colour, [first + i * step + n for n in range(step)])
            return carry

        lax.fori_loop(0, count // step, some_planes, 0)

    def inner(r):
        sweep_range(r, 0, low_edge + 1, top)
        sweep_range(r, 1, low_edge + 2, top - 1)

    def outer(r):
        half_sweep(r, 0, [low_edge - 1, low_edge, top, top + 1])
        half_sweep(r, 1, [low_edge, low_edge + 1, top - 1, top])

    def advance(r, e):
        if skips(r, e):
            take_far(r, e - 1)
            for colour in range(2):
                pl.when(far_below)(functools.partial(half_sweep, r, colour, [low_edge - 3 + colour, low_edge - 2 + colour]))
                pl.when(far_above)(functools.partial(half_sweep, r, colour, [top + 2 - colour, top + 3 - colour]))
        take_halo(r, e)
        outer(r)
        if e < rounds - 1:
            send_halo(r, e + 1)
            if far and r >= pairs and e % 2 == 1:
                send_far(r, e + 1)
        elif 1 <= r < pairs:
            for n in range(len(remote)):
                for i in range(len(early), len(pieces)):
                    result_copy(n, r, i).start()

    def prepare(r, e):
        inner(r)
        if e == rounds - 1 and 1 <= r < pairs:
            for n in range(len(remote)):
                for i in range(len(early)):
                    result_copy(n, r, i).start()

    def settle(n, i):
        copy = raw_copy(n, i)
        copy.wait_recv()
        start, count = spans[i]

        def plane(p, carry):
            for c in range(2):
                for k in range(comps):
                    work[pairs + n, c, p + edge, k] = raw[pairs + n, c, p, k]
            return carry

        lax.fori_loop(start, start + count, plane, 0)

    for n in range(len(remote)):
        for i in range(2):
            raw_copy(n, i).start()
    own = list(range(pairs - 1, -1, -1))
    send_halo(own[0], 0)
    for copy in bond_copies:
        copy.start()
    if far:
        for side, copy in far_bonds:
            pl.when((far_above, far_below)[side])(copy.start)
    for n in range(len(remote)):
        raw_copy(n, 2).start()
    lax.fori_loop(1, planes, own_bonds, 0)
    for r in own[1:]:
        send_halo(r, 0)
    for r in own:
        inner(r)
    for copy in bond_copies:
        copy.wait()
    bonds_of(edge - 1, low[0, 1], low[1, 1], low[2, 1], low[2, 0])
    bonds_of(edge, coup[0, 0], coup[1, 0], coup[2, 0], low[2, 1])
    bonds_of(edge + planes, high[0], high[1], high[2], coup[2, planes - 1])

    advance(own[0], 0)
    for n, g in enumerate(guests):
        settle(n, 0)
        settle(n, 1)
        send_halo(g, 0)
    for r in own[1:]:
        advance(r, 0)
    for r in own:
        prepare(r, 1)
    if far:
        take_far_bonds()

    advance(own[0], 1)
    prepare(own[0], 2)
    for n, g in enumerate(guests):
        settle(n, 2)
        if far:
            send_far(g, 0)
    for g in guests:
        inner(g)
        advance(g, 0)
        prepare(g, 1)
    for r in own[1:]:
        advance(r, 1)
        prepare(r, 2)
    for e in range(2, rounds):
        for r in own[:1] + guests + own[1:]:
            late = e - 1 if r in guests else e
            advance(r, late)
            if late < rounds - 1:
                prepare(r, late + 1)

    def write(j, count, place):
        if j in remote:
            n = remote.index(j)
            given = lambda r, p, c, k: res[n, r - 1, c, p, k] if r else work[pairs + n, c, p + edge, k]
        else:
            given = lambda r, p, c, k: work[r, c, p + edge, k]

        def write_plane(i, carry):
            p = place(i)
            mask = front(p + edge)
            for slot in (2 * j, 2 * j + 1):
                pair = lax.rem(source[group * rep_dev + slot], rep_dev) // 2
                for k in range(comps):
                    colours = []
                    for c in range(2):
                        value = given(0, p, c, k)
                        for r in range(1, pairs):
                            value = jnp.where(pair == r, given(r, p, c, k), value)
                        colours.append(jnp.where(kept[slot], work[j, c, p + edge, k], value))
                    zero, one = colours
                    out[slot, k, p, :half] = jnp.where(mask, zero, one)
                    out[slot, k, p, half:] = reverse_rows(jnp.where(mask, one, zero), row)
            return carry

        lax.fori_loop(0, count, write_plane, 0)

    middle = (planes - 2 * WIDTH, lambda i: i + WIDTH)
    outside = (2 * WIDTH, lambda i: i + i // WIDTH * (planes - 2 * WIDTH))
    for j in range(pairs):
        if j not in remote:
            write(j, planes, lambda i: i)
    for n in range(len(remote)):
        for r in range(1, pairs):
            for i in range(len(early)):
                result_copy(n, r, i).wait()
    for j in remote:
        write(j, *middle)
    for g in guests:
        advance(g, rounds - 1)
    for n in range(len(remote)):
        for i in range(3):
            raw_copy(n, i).wait_send()
        for r in range(1, pairs):
            for i in range(len(early), len(pieces)):
                result_copy(n, r, i).wait()
    for j in remote:
        write(j, *outside)


def solution(mesh):
    n_rep, n_slab = mesh.shape["rep"], mesh.shape["slab"]

    def local(spins, couplings, source):
        rep_dev, comps, planes, rows, cols = spins.shape
        pairs, half = rep_dev // 2, rows // 2
        n_remote = sum(1 for j in range(pairs) if (1 + j) % n_rep)
        depth = min(FAR, planes)
        spare = max(depth - WIDTH, 1)
        deep = planes + 2 * depth
        starts = pairs + n_remote
        f32, i32, dma = jnp.float32, jnp.int32, pltpu.SemaphoreType.DMA
        return pl.pallas_call(
            functools.partial(kernel, n_rep, n_slab),
            out_shape=pltpu.VMEM(spins.shape, f32),
            in_specs=[
                pl.BlockSpec(memory_space=pltpu.SMEM),
                pl.BlockSpec(memory_space=pl.ANY),
                pl.BlockSpec(memory_space=pl.ANY),
            ],
            out_specs=pl.BlockSpec(memory_space=pltpu.VMEM),
            scratch_shapes=[
                pltpu.VMEM(spins.shape, f32),
                pltpu.VMEM(couplings.shape, i32),
                pltpu.VMEM((starts, 2, planes, comps, half, cols), f32),
                pltpu.VMEM((starts, 2, deep, comps, half, cols), f32),
                pltpu.VMEM((deep, 2, 6, half, cols), f32),
                pltpu.VMEM((3, WIDTH, rows, cols), i32),
                pltpu.VMEM((3, rows, cols), i32),
                pltpu.VMEM((3, spare + 1, rows, cols), i32),
                pltpu.VMEM((3, spare, rows, cols), i32),
                pltpu.VMEM((max(n_remote, 1), pairs - 1, 2, planes, comps, half, cols), f32),
                pltpu.VMEM((starts, SWEEPS, 2, WIDTH + 1, comps, half, cols), f32),
                pltpu.VMEM((starts, (SWEEPS + 1) // 2, 2, 2, spare, comps, half, cols), f32),
                pltpu.VMEM((starts, max((SWEEPS - 1) // 2, 1), 2, 2, spare, comps, half, cols), f32),
                dma((6,)),
                dma((6,)),
                dma((starts, SWEEPS, 2, 2)),
                dma((starts, SWEEPS, 2, 2)),
                dma((starts, (SWEEPS + 1) // 2, 2, 2)),
                dma((starts, (SWEEPS + 1) // 2, 2, 2)),
                dma((max(n_remote, 1), 3)),
                dma((max(n_remote, 1), 3)),
                dma((max(n_remote, 1), pairs - 1, 6)),
                dma((max(n_remote, 1), pairs - 1, 6)),
                dma((pairs + 1,)),
            ],
            compiler_params=pltpu.CompilerParams(collective_id=0, has_side_effects=True),
        )(source, spins, couplings)

    in_specs = (P("rep", None, "slab", None, None), P(None, "slab", None, None), P())
    out_specs = P("rep", None, "slab", None, None)
    return jax.shard_map(local, mesh=mesh, in_specs=in_specs, out_specs=out_specs, check_vma=False)
```

```python
import functools

import jax
import jax.numpy as jnp
from jax import lax
from jax.experimental import pallas as pl
from jax.experimental.pallas import tpu as pltpu
from jax.sharding import PartitionSpec as P

SWEEPS = 4
GROUP = 5
WIDTH = 2
FAR = 4
MESH = pl.DeviceIdType.MESH


def reverse_rows(value, row):
    count = value.shape[0]
    shift = 1
    while shift < count:
        down = pltpu.roll(value, shift, 0)
        if 2 * shift == count:
            value = down
        else:
            value = jnp.where((row & shift) == 0, pltpu.roll(value, count - shift, 0), down)
        shift *= 2
    return value


def kernel(n_rep, n_slab, source, spins_hbm, coup_hbm, out, spins, coup, raw, work, bonds, low, high, low_far, high_far, res, land, land_far, stage, c_send, c_recv, h_send, h_recv, x_send, x_recv, r_send, r_recv, m_send, m_recv, in_sem):
    rep_dev, comps, planes, rows, cols = spins.shape
    pairs, half, rounds = rep_dev // 2, rows // 2, SWEEPS
    edge = work.shape[2] - planes >> 1
    depth = min(FAR, edge)
    group, slab = lax.axis_index("rep"), lax.axis_index("slab")
    up, down = lax.rem(slab + 1, n_slab), lax.rem(slab + n_slab - 1, n_slab)
    far = depth > WIDTH
    far_below, far_above = slab == 0, up == 0
    offsets = [(1 + j) % n_rep for j in range(pairs)]
    remote = [j for j in range(pairs) if offsets[j]]
    guests = [pairs + n for n in range(len(remote))]
    loads = [pltpu.make_async_copy(spins_hbm.at[pl.ds(2 * r, 2)], spins.at[pl.ds(2 * r, 2)], in_sem.at[r]) for r in range(pairs)]
    loads.append(pltpu.make_async_copy(coup_hbm, coup, in_sem.at[pairs]))
    barrier = pltpu.get_barrier_semaphore()
    for side in (up, down):
        pl.semaphore_signal(barrier, inc=1, device_id=(group, side), device_id_type=MESH)
    for j in remote:
        giver = lax.rem(group + offsets[j], n_rep)
        pl.semaphore_signal(barrier, inc=1, device_id=(giver, slab), device_id_type=MESH)

    for copy in loads:
        copy.start()

    row = lax.broadcasted_iota(jnp.int32, (half, cols), 0)
    site = row + lax.broadcasted_iota(jnp.int32, (half, cols), 1)

    def front(plane):
        return ((site + (slab * planes + plane + edge)) & 1) == 0

    def pack(mask, first, second):
        second = reverse_rows(second, row)
        return jnp.where(mask, first, second), jnp.where(mask, second, first)

    def remote_copy(src, dst, send, recv, device):
        return pltpu.make_async_remote_copy(
            src_ref=src, dst_ref=dst, send_sem=send, recv_sem=recv, device_id=device, device_id_type=MESH
        )

    def when(condition, action):
        if condition is None:
            action()
        else:
            pl.when(condition)(action)

    def halo_copies(r, e, side):
        start, near, device = ((edge + planes - WIDTH, edge + planes - 1, up), (edge, edge, down))[side]
        copies = [remote_copy(
            work.at[r, 1, pl.ds(start, WIDTH)], land.at[r, e, side, pl.ds(0, WIDTH)],
            h_send.at[r, e, side, 0], h_recv.at[r, e, side, 0], (group, device),
        )]
        if e == 0:
            copies.append(remote_copy(
                work.at[r, 0, near], land.at[r, e, side, WIDTH],
                h_send.at[r, e, side, 1], h_recv.at[r, e, side, 1], (group, device),
            ))
        return copies

    def deepens(r, e):
        return far and e % 2 == 0 and r >= 1 and 0 < e == rounds - 2

    def skips(r, e):
        return e % 2 == 1 and deepens(r, e - 1)

    def send_halo(r, e, sides=(0, 1)):
        for side in sides:
            for copy in halo_copies(r, e, side):
                when(jnp.logical_not((far_above, far_below)[side]) if skips(r, e) else None, copy.start)

    def take_halo(r, e, side):
        near_side = jnp.logical_not((far_below, far_above)[side]) if skips(r, e) else None
        for copy in halo_copies(r, e, 1 - side):
            when(near_side, copy.wait_send)

        def take():
            for copy in halo_copies(r, e, side):
                copy.wait_recv()
            start, near = ((edge - WIDTH, edge - 1), (edge + planes, edge + planes))[side]
            for k in range(comps):
                for d in range(WIDTH):
                    work[r, 1, start + d, k] = land[r, e, side, d, k]
                if e == 0:
                    work[r, 0, near, k] = land[r, e, side, WIDTH, k]

        when(near_side, take)

    def far_starts(side):
        return ((planes - depth + 1, planes - depth), (1, WIDTH))[side]

    def far_copies(r, e, side):
        device = (up, down)[side]
        spare = depth - WIDTH
        return [
            remote_copy(
                stage.at[r, e // 2 - 1, side, c] if e else raw.at[r, c, pl.ds(far_starts(side)[c], spare)],
                land_far.at[r, e // 2, side, c], x_send.at[r, e // 2, side, c], x_recv.at[r, e // 2, side, c],
                (group, device),
            )
            for c in range(2)
        ]

    def send_far(r, e, sides=(0, 1)):
        for side in sides:
            def send(side=side):
                if e:
                    for c in range(2):
                        for d in range(depth - WIDTH):
                            for k in range(comps):
                                stage[r, e // 2 - 1, side, c, d, k] = work[r, c, edge + far_starts(side)[c] + d, k]
                for copy in far_copies(r, e, side):
                    copy.start()
            pl.when((far_above, far_below)[side])(send)

    def take_far(r, e, side):
        def take():
            for copy in far_copies(r, e, 1 - side):
                copy.wait_send()
            starts = ((edge - depth + 1, edge - depth), (edge + planes + 1, edge + planes + WIDTH))[side]
            for copy in far_copies(r, e, side):
                copy.wait_recv()
            for c in range(2):
                for d in range(depth - WIDTH):
                    for k in range(comps):
                        work[r, c, starts[c] + d, k] = land_far[r, e // 2, side, c, d, k]
            for colour in range(2):
                first = (low_edge - 3 + colour, top + 2 - colour)[side]
                half_sweep(r, colour, [first, first + 1])

        pl.when((far_below, far_above)[side])(take)

    kept = []
    for slot in range(rep_dev):
        own = group * rep_dev + slot
        kept.append(source[own] == own)

    for r in range(pairs):
        loads[r].wait()

        def pack_plane(p, carry, r=r):
            mask = front(p + edge)
            for k in range(comps):
                value = jnp.where(kept[2 * r], spins[2 * r, k, p], spins[2 * r + 1, k, p])
                for c, part in enumerate(pack(mask, value[:half], value[half:])):
                    work[r, c, p + edge, k] = part
                    raw[r, c, p, k] = part
            return carry

        lax.fori_loop(0, planes, pack_plane, 0)

    def bonds_of(plane, jx, jy, jz, jz_below):
        mask = front(plane)
        jx, jy, jz, jz_below = [(2 * j - 1).astype(jnp.float32) for j in (jx, jy, jz, jz_below)]
        jw = pltpu.roll(jx, 1, 1)
        first, second = jy[:half], jy[half:]
        south_first = jnp.where(row == 0, second[half - 1 :], pltpu.roll(first, 1, 0))
        south_second = jnp.where(row == 0, first[half - 1 :], pltpu.roll(second, 1, 0))
        first_r = reverse_rows(second, row)
        south_r = reverse_rows(south_second, row)
        east = pack(mask, jx[:half], jx[half:])
        west = pack(mask, jw[:half], jw[half:])
        upper = pack(mask, jz[:half], jz[half:])
        lower = pack(mask, jz_below[:half], jz_below[half:])
        after = (jnp.where(mask, first, south_r), jnp.where(mask, south_r, first))
        before = (jnp.where(mask, south_first, first_r), jnp.where(mask, first_r, south_first))
        for i, bond in enumerate((east, west, after, before, upper, lower)):
            for c in range(2):
                bonds[plane, c, i] = bond[c]

    def own_bonds(p, carry):
        bonds_of(p + edge, coup[0, p], coup[1, p], coup[2, p], coup[2, p - 1])
        return carry

    loads[pairs].wait()
    pl.semaphore_wait(barrier, 2 + len(remote))

    rest = [(0, 1, planes - 2), (1, WIDTH, planes - 2 * WIDTH)]
    outer_parts = [(1, 0, WIDTH), (1, planes - WIDTH, WIDTH), (0, 0, 1), (0, planes - 1, 1)]
    pieces = outer_parts + rest
    sent = range(len(outer_parts))
    kept_back = range(len(outer_parts), len(pieces))

    def raw_copy(n, i):
        taker = lax.rem(group + n_rep - offsets[remote[n]], n_rep)
        c, start, count = pieces[i]
        span = pl.ds(start, count)
        return remote_copy(raw.at[0, c, span], raw.at[pairs + n, c, span], r_send.at[n, i], r_recv.at[n, i], (taker, slab))

    def result_copy(n, r, i):
        taker = lax.rem(group + n_rep - offsets[remote[n]], n_rep)
        c, start, count = pieces[i]
        return remote_copy(
            work.at[r, c, pl.ds(start + edge, count)], res.at[n, r - 1, c, pl.ds(start, count)],
            m_send.at[n, r - 1, i], m_recv.at[n, r - 1, i], (taker, slab),
        )

    bond_copies = [
        remote_copy(coup.at[2, planes - WIDTH], low.at[2, 0], c_send.at[0], c_recv.at[0], (group, up)),
        remote_copy(coup.at[:, planes - 1], low.at[:, 1], c_send.at[1], c_recv.at[1], (group, up)),
        remote_copy(coup.at[:, 0], high, c_send.at[2], c_recv.at[2], (group, down)),
    ]
    far_bonds = []
    if far:
        far_bonds = [
            (0, remote_copy(coup.at[2, planes - depth], low_far.at[2, 0], c_send.at[3], c_recv.at[3], (group, up))),
            (0, remote_copy(coup.at[:, planes - depth + 1 : planes - 1], low_far.at[:, 1:], c_send.at[4], c_recv.at[4], (group, up))),
            (1, remote_copy(coup.at[:, 1 : depth - 1], high_far, c_send.at[5], c_recv.at[5], (group, down))),
        ]
    def take_far_bonds():
        for side, copy in far_bonds:
            pl.when((far_above, far_below)[side])(copy.wait_send)

        def below():
            for side, copy in far_bonds:
                if side == 0:
                    copy.wait_recv()

            def plane(i, carry):
                bonds_of(edge - depth + i, low_far[0, i], low_far[1, i], low_far[2, i], low_far[2, i - 1])
                return carry

            lax.fori_loop(1, depth - 1, plane, 0)

        def above():
            for side, copy in far_bonds:
                if side == 1:
                    copy.wait_recv()
            bonds_of(edge + planes + 1, high_far[0, 0], high_far[1, 0], high_far[2, 0], high[2])

            def plane(i, carry):
                bonds_of(edge + planes + 1 + i, high_far[0, i], high_far[1, i], high_far[2, i], high_far[2, i - 1])
                return carry

            lax.fori_loop(1, depth - 2, plane, 0)

        pl.when(far_below)(below)
        pl.when(far_above)(above)

    def half_sweep(r, colour, parts):
        other = 1 - colour

        def turned(p):
            east, west, after, before, upper, lower = [bonds[p, colour, i] for i in range(6)]
            field, spin = [], []
            for k in range(comps):
                q = work[r, other, p, k]
                north = jnp.where(row == half - 1, q, pltpu.roll(q, half - 1, 0))
                south = jnp.where(row == 0, q, pltpu.roll(q, 1, 0))
                h = east * pltpu.roll(q, cols - 1, 1) + west * pltpu.roll(q, 1, 1)
                h = h + after * north + before * south
                h = h + upper * work[r, other, p + 1, k] + lower * work[r, other, p - 1, k]
                field.append(h)
                spin.append(work[r, colour, p, k])
            along = sum(s * h for s, h in zip(spin, field))
            strength = sum(h * h for h in field)
            scale = 2.0 * along / jnp.maximum(strength, 1.0)
            return [scale * h - s for s, h in zip(spin, field)]

        planes_of = list(parts)
        new = [turned(p) for p in planes_of]
        for p, value in zip(planes_of, new):
            for k in range(comps):
                work[r, colour, p, k] = value[k]

    low_edge, top = edge, edge + planes - 1

    def sweep_range(r, colour, first, last):
        count = last - first
        step = max(g for g in range(1, GROUP + 1) if count % g == 0)

        def some_planes(i, carry):
            half_sweep(r, colour, [first + i * step + n for n in range(step)])
            return carry

        lax.fori_loop(0, count // step, some_planes, 0)

    def inner(r):
        sweep_range(r, 0, low_edge + 1, top)
        sweep_range(r, 1, low_edge + 2, top - 1)

    def outer(r, side):
        half_sweep(r, 0, ([low_edge - 1, low_edge], [top, top + 1])[side])
        half_sweep(r, 1, ([low_edge, low_edge + 1], [top - 1, top])[side])

    def advance(r, e):
        for side in (1, 0):
            if skips(r, e):
                take_far(r, e - 1, side)
            take_halo(r, e, side)
            outer(r, side)
            if e < rounds - 1:
                send_halo(r, e + 1, (1 - side,))
                if deepens(r, e + 1):
                    send_far(r, e + 1, (1 - side,))
            elif 1 <= r < pairs:
                for n in range(len(remote)):
                    for i in ((0, 2), (1, 3))[side]:
                        result_copy(n, r, i).start()

    def prepare(r, e):
        inner(r)
        if e == rounds - 1 and 1 <= r < pairs:
            for n in range(len(remote)):
                for i in kept_back:
                    result_copy(n, r, i).start()

    def settle(n, parts):
        for i in parts:
            raw_copy(n, i).wait_recv()
        for i in parts:
            c, start, count = pieces[i]
            for p in range(start, start + count):
                for k in range(comps):
                    work[pairs + n, c, p + edge, k] = raw[pairs + n, c, p, k]

    own = list(range(pairs - 1, -1, -1))
    send_halo(own[0], 0)
    for copy in bond_copies:
        copy.start()
    for n in range(len(remote)):
        for i in sent:
            raw_copy(n, i).start()
    if far:
        for side, copy in far_bonds:
            pl.when((far_above, far_below)[side])(copy.start)
    for n in range(len(remote)):
        for i in kept_back:
            raw_copy(n, i).start()
    lax.fori_loop(1, planes, own_bonds, 0)
    for r in own[1:]:
        send_halo(r, 0)
    for r in own:
        inner(r)
    for copy in bond_copies:
        copy.wait()
    bonds_of(edge - 1, low[0, 1], low[1, 1], low[2, 1], low[2, 0])
    bonds_of(edge, coup[0, 0], coup[1, 0], coup[2, 0], low[2, 1])
    bonds_of(edge + planes, high[0], high[1], high[2], coup[2, planes - 1])

    advance(own[0], 0)
    for n, g in enumerate(guests):
        settle(n, sent)
        send_halo(g, 0)
    for r in own[1:]:
        advance(r, 0)
    for r in own:
        prepare(r, 1)
    if far:
        take_far_bonds()

    advance(own[0], 1)
    prepare(own[0], 2)
    for n, g in enumerate(guests):
        settle(n, kept_back)
    for g in guests:
        inner(g)
        advance(g, 0)
        prepare(g, 1)
    for r in own[1:]:
        advance(r, 1)
        prepare(r, 2)
    for e in range(2, rounds):
        for r in own[:1] + guests + own[1:]:
            late = e - 1 if r in guests else e
            advance(r, late)
            if late < rounds - 1:
                prepare(r, late + 1)

    def write(j, count, place):
        if j in remote:
            n = remote.index(j)
            given = lambda r, p, c, k: res[n, r - 1, c, p, k] if r else work[pairs + n, c, p + edge, k]
        else:
            given = lambda r, p, c, k: work[r, c, p + edge, k]

        def write_plane(i, carry):
            p = place(i)
            mask = front(p + edge)
            for slot in (2 * j, 2 * j + 1):
                pair = lax.rem(source[group * rep_dev + slot], rep_dev) // 2
                for k in range(comps):
                    colours = []
                    for c in range(2):
                        value = given(0, p, c, k)
                        for r in range(1, pairs):
                            value = jnp.where(pair == r, given(r, p, c, k), value)
                        colours.append(jnp.where(kept[slot], work[j, c, p + edge, k], value))
                    zero, one = colours
                    out[slot, k, p, :half] = jnp.where(mask, zero, one)
                    out[slot, k, p, half:] = reverse_rows(jnp.where(mask, one, zero), row)
            return carry

        lax.fori_loop(0, count, write_plane, 0)

    middle = (planes - 2 * WIDTH, lambda i: i + WIDTH)
    outside = (2 * WIDTH, lambda i: i + i // WIDTH * (planes - 2 * WIDTH))
    for j in range(pairs):
        if j not in remote:
            write(j, planes, lambda i: i)
    for n in range(len(remote)):
        for r in range(1, pairs):
            for i in kept_back:
                result_copy(n, r, i).wait()
    for j in remote:
        write(j, *middle)
    for g in guests:
        advance(g, rounds - 1)
    for n in range(len(remote)):
        for i in range(len(pieces)):
            raw_copy(n, i).wait_send()
        for r in range(1, pairs):
            for i in sent:
                result_copy(n, r, i).wait()
    for j in remote:
        write(j, *outside)


def solution(mesh):
    n_rep, n_slab = mesh.shape["rep"], mesh.shape["slab"]

    def local(spins, couplings, source):
        rep_dev, comps, planes, rows, cols = spins.shape
        pairs, half = rep_dev // 2, rows // 2
        n_remote = sum(1 for j in range(pairs) if (1 + j) % n_rep)
        depth = min(FAR, planes)
        spare = max(depth - WIDTH, 1)
        deep = planes + 2 * depth
        starts = pairs + n_remote
        f32, i32, dma = jnp.float32, jnp.int32, pltpu.SemaphoreType.DMA
        return pl.pallas_call(
            functools.partial(kernel, n_rep, n_slab),
            out_shape=pltpu.VMEM(spins.shape, f32),
            in_specs=[
                pl.BlockSpec(memory_space=pltpu.SMEM),
                pl.BlockSpec(memory_space=pl.ANY),
                pl.BlockSpec(memory_space=pl.ANY),
            ],
            out_specs=pl.BlockSpec(memory_space=pltpu.VMEM),
            scratch_shapes=[
                pltpu.VMEM(spins.shape, f32),
                pltpu.VMEM(couplings.shape, i32),
                pltpu.VMEM((starts, 2, planes, comps, half, cols), f32),
                pltpu.VMEM((starts, 2, deep, comps, half, cols), f32),
                pltpu.VMEM((deep, 2, 6, half, cols), f32),
                pltpu.VMEM((3, WIDTH, rows, cols), i32),
                pltpu.VMEM((3, rows, cols), i32),
                pltpu.VMEM((3, spare + 1, rows, cols), i32),
                pltpu.VMEM((3, spare, rows, cols), i32),
                pltpu.VMEM((max(n_remote, 1), pairs - 1, 2, planes, comps, half, cols), f32),
                pltpu.VMEM((starts, SWEEPS, 2, WIDTH + 1, comps, half, cols), f32),
                pltpu.VMEM((starts, (SWEEPS + 1) // 2, 2, 2, spare, comps, half, cols), f32),
                pltpu.VMEM((starts, max((SWEEPS - 1) // 2, 1), 2, 2, spare, comps, half, cols), f32),
                dma((6,)),
                dma((6,)),
                dma((starts, SWEEPS, 2, 2)),
                dma((starts, SWEEPS, 2, 2)),
                dma((starts, (SWEEPS + 1) // 2, 2, 2)),
                dma((starts, (SWEEPS + 1) // 2, 2, 2)),
                dma((max(n_remote, 1), 6)),
                dma((max(n_remote, 1), 6)),
                dma((max(n_remote, 1), pairs - 1, 6)),
                dma((max(n_remote, 1), pairs - 1, 6)),
                dma((pairs + 1,)),
            ],
            compiler_params=pltpu.CompilerParams(collective_id=0, has_side_effects=True),
        )(source, spins, couplings)

    in_specs = (P("rep", None, "slab", None, None), P(None, "slab", None, None), P())
    out_specs = P("rep", None, "slab", None, None)
    return jax.shard_map(local, mesh=mesh, in_specs=in_specs, out_specs=out_specs, check_vma=False)
```

```python
import functools

import jax
import jax.numpy as jnp
from jax import lax
from jax.experimental import pallas as pl
from jax.experimental.pallas import tpu as pltpu
from jax.sharding import PartitionSpec as P

SWEEPS = 4
GROUP = 5
WIDTH = 2
FAR = 4
MESH = pl.DeviceIdType.MESH


def reverse_rows(value, row):
    count = value.shape[0]
    shift = 1
    while shift < count:
        down = pltpu.roll(value, shift, 0)
        if 2 * shift == count:
            value = down
        else:
            value = jnp.where((row & shift) == 0, pltpu.roll(value, count - shift, 0), down)
        shift *= 2
    return value


def kernel(n_rep, n_slab, source, spins_hbm, coup_hbm, out, spins, coup, raw, work, bonds, low, high, low_far, high_far, res, land, land_far, stage, c_send, c_recv, h_send, h_recv, x_send, x_recv, r_send, r_recv, m_send, m_recv, in_sem):
    rep_dev, comps, planes, rows, cols = spins.shape
    pairs, half, rounds = rep_dev // 2, rows // 2, SWEEPS
    edge = work.shape[2] - planes >> 1
    depth = min(FAR, edge)
    group, slab = lax.axis_index("rep"), lax.axis_index("slab")
    up, down = lax.rem(slab + 1, n_slab), lax.rem(slab + n_slab - 1, n_slab)
    far = depth > WIDTH
    far_below, far_above = slab == 0, up == 0
    offsets = [(1 + j) % n_rep for j in range(pairs)]
    remote = [j for j in range(pairs) if offsets[j]]
    guests = [pairs + n for n in range(len(remote))]
    loads = [pltpu.make_async_copy(spins_hbm.at[pl.ds(2 * r, 2)], spins.at[pl.ds(2 * r, 2)], in_sem.at[r]) for r in range(pairs)]
    loads.append(pltpu.make_async_copy(coup_hbm, coup, in_sem.at[pairs]))
    barrier = pltpu.get_barrier_semaphore()
    for side in (up, down):
        pl.semaphore_signal(barrier, inc=1, device_id=(group, side), device_id_type=MESH)
    for j in remote:
        giver = lax.rem(group + offsets[j], n_rep)
        pl.semaphore_signal(barrier, inc=1, device_id=(giver, slab), device_id_type=MESH)

    for copy in loads:
        copy.start()

    row = lax.broadcasted_iota(jnp.int32, (half, cols), 0)
    site = row + lax.broadcasted_iota(jnp.int32, (half, cols), 1)

    def front(plane):
        return ((site + (slab * planes + plane + edge)) & 1) == 0

    def pack(mask, first, second):
        second = reverse_rows(second, row)
        return jnp.where(mask, first, second), jnp.where(mask, second, first)

    def remote_copy(src, dst, send, recv, device):
        return pltpu.make_async_remote_copy(
            src_ref=src, dst_ref=dst, send_sem=send, recv_sem=recv, device_id=device, device_id_type=MESH
        )

    def when(condition, action):
        if condition is None:
            action()
        else:
            pl.when(condition)(action)

    def halo_copies(r, e, side):
        start, near, device = ((edge + planes - WIDTH, edge + planes - 1, up), (edge, edge, down))[side]
        copies = [remote_copy(
            work.at[r, 1, pl.ds(start, WIDTH)], land.at[r, e, side, pl.ds(0, WIDTH)],
            h_send.at[r, e, side, 0], h_recv.at[r, e, side, 0], (group, device),
        )]
        if e == 0:
            copies.append(remote_copy(
                work.at[r, 0, near], land.at[r, e, side, WIDTH],
                h_send.at[r, e, side, 1], h_recv.at[r, e, side, 1], (group, device),
            ))
        return copies

    def deepens(r, e):
        return far and e % 2 == 0 and r >= 1 and 0 < e == rounds - 2

    def skips(r, e):
        return e % 2 == 1 and deepens(r, e - 1)

    def send_halo(r, e, sides=(0, 1)):
        for side in sides:
            for copy in halo_copies(r, e, side):
                when(jnp.logical_not((far_above, far_below)[side]) if skips(r, e) else None, copy.start)

    def take_halo(r, e, side):
        near_side = jnp.logical_not((far_below, far_above)[side]) if skips(r, e) else None
        for copy in halo_copies(r, e, 1 - side):
            when(near_side, copy.wait_send)

        def take():
            for copy in halo_copies(r, e, side):
                copy.wait_recv()
            start, near = ((edge - WIDTH, edge - 1), (edge + planes, edge + planes))[side]
            for k in range(comps):
                for d in range(WIDTH):
                    work[r, 1, start + d, k] = land[r, e, side, d, k]
                if e == 0:
                    work[r, 0, near, k] = land[r, e, side, WIDTH, k]

        when(near_side, take)

    def far_starts(side):
        return ((planes - depth + 1, planes - depth), (1, WIDTH))[side]

    def far_copies(r, e, side):
        device = (up, down)[side]
        spare = depth - WIDTH
        return [
            remote_copy(
                stage.at[r, e // 2 - 1, side, c] if e else raw.at[r, c, pl.ds(far_starts(side)[c], spare)],
                land_far.at[r, e // 2, side, c], x_send.at[r, e // 2, side, c], x_recv.at[r, e // 2, side, c],
                (group, device),
            )
            for c in range(2)
        ]

    def send_far(r, e, sides=(0, 1)):
        for side in sides:
            def send(side=side):
                if e:
                    for c in range(2):
                        for d in range(depth - WIDTH):
                            for k in range(comps):
                                stage[r, e // 2 - 1, side, c, d, k] = work[r, c, edge + far_starts(side)[c] + d, k]
                for copy in far_copies(r, e, side):
                    copy.start()
            pl.when((far_above, far_below)[side])(send)

    def take_far(r, e, side):
        def take():
            for copy in far_copies(r, e, 1 - side):
                copy.wait_send()
            starts = ((edge - depth + 1, edge - depth), (edge + planes + 1, edge + planes + WIDTH))[side]
            for copy in far_copies(r, e, side):
                copy.wait_recv()
            for c in range(2):
                for d in range(depth - WIDTH):
                    for k in range(comps):
                        work[r, c, starts[c] + d, k] = land_far[r, e // 2, side, c, d, k]
            for colour in range(2):
                first = (low_edge - 3 + colour, top + 2 - colour)[side]
                half_sweep(r, colour, [first, first + 1])

        pl.when((far_below, far_above)[side])(take)

    kept = []
    for slot in range(rep_dev):
        own = group * rep_dev + slot
        kept.append(source[own] == own)

    for r in range(pairs):
        loads[r].wait()

        def pack_plane(p, carry, r=r):
            mask = front(p + edge)
            for k in range(comps):
                value = jnp.where(kept[2 * r], spins[2 * r, k, p], spins[2 * r + 1, k, p])
                for c, part in enumerate(pack(mask, value[:half], value[half:])):
                    work[r, c, p + edge, k] = part
                    raw[r, c, p, k] = part
            return carry

        lax.fori_loop(0, planes, pack_plane, 0)

    def bonds_of(plane, jx, jy, jz, jz_below):
        mask = front(plane)
        jx, jy, jz, jz_below = [(2 * j - 1).astype(jnp.float32) for j in (jx, jy, jz, jz_below)]
        jw = pltpu.roll(jx, 1, 1)
        first, second = jy[:half], jy[half:]
        south_first = jnp.where(row == 0, second[half - 1 :], pltpu.roll(first, 1, 0))
        south_second = jnp.where(row == 0, first[half - 1 :], pltpu.roll(second, 1, 0))
        first_r = reverse_rows(second, row)
        south_r = reverse_rows(south_second, row)
        east = pack(mask, jx[:half], jx[half:])
        west = pack(mask, jw[:half], jw[half:])
        upper = pack(mask, jz[:half], jz[half:])
        lower = pack(mask, jz_below[:half], jz_below[half:])
        after = (jnp.where(mask, first, south_r), jnp.where(mask, south_r, first))
        before = (jnp.where(mask, south_first, first_r), jnp.where(mask, first_r, south_first))
        for i, bond in enumerate((east, west, after, before, upper, lower)):
            for c in range(2):
                bonds[plane, c, i] = bond[c]

    def own_bonds(p, carry):
        bonds_of(p + edge, coup[0, p], coup[1, p], coup[2, p], coup[2, p - 1])
        return carry

    loads[pairs].wait()
    pl.semaphore_wait(barrier, 2 + len(remote))

    rest = [(0, 1, planes - 2), (1, WIDTH, planes - 2 * WIDTH)]
    outer_parts = [(1, 0, WIDTH), (1, planes - WIDTH, WIDTH), (0, 0, 1), (0, planes - 1, 1)]
    pieces = outer_parts + rest
    sent = range(len(outer_parts))
    kept_back = range(len(outer_parts), len(pieces))

    def raw_copy(n, i):
        taker = lax.rem(group + n_rep - offsets[remote[n]], n_rep)
        c, start, count = pieces[i]
        span = pl.ds(start, count)
        return remote_copy(raw.at[0, c, span], raw.at[pairs + n, c, span], r_send.at[n, i], r_recv.at[n, i], (taker, slab))

    def result_copy(n, r, i):
        taker = lax.rem(group + n_rep - offsets[remote[n]], n_rep)
        c, start, count = pieces[i]
        return remote_copy(
            work.at[r, c, pl.ds(start + edge, count)], res.at[n, r - 1, c, pl.ds(start, count)],
            m_send.at[n, r - 1, i], m_recv.at[n, r - 1, i], (taker, slab),
        )

    bond_copies = [
        remote_copy(coup.at[2, planes - WIDTH], low.at[2, 0], c_send.at[0], c_recv.at[0], (group, up)),
        remote_copy(coup.at[:, planes - 1], low.at[:, 1], c_send.at[1], c_recv.at[1], (group, up)),
        remote_copy(coup.at[:, 0], high, c_send.at[2], c_recv.at[2], (group, down)),
    ]
    far_bonds = []
    if far:
        far_bonds = [
            (0, remote_copy(coup.at[2, planes - depth], low_far.at[2, 0], c_send.at[3], c_recv.at[3], (group, up))),
            (0, remote_copy(coup.at[:, planes - depth + 1 : planes - 1], low_far.at[:, 1:], c_send.at[4], c_recv.at[4], (group, up))),
            (1, remote_copy(coup.at[:, 1 : depth - 1], high_far, c_send.at[5], c_recv.at[5], (group, down))),
        ]
    def take_far_bonds():
        for side, copy in far_bonds:
            pl.when((far_above, far_below)[side])(copy.wait_send)

        def below():
            for side, copy in far_bonds:
                if side == 0:
                    copy.wait_recv()

            def plane(i, carry):
                bonds_of(edge - depth + i, low_far[0, i], low_far[1, i], low_far[2, i], low_far[2, i - 1])
                return carry

            lax.fori_loop(1, depth - 1, plane, 0)

        def above():
            for side, copy in far_bonds:
                if side == 1:
                    copy.wait_recv()
            bonds_of(edge + planes + 1, high_far[0, 0], high_far[1, 0], high_far[2, 0], high[2])

            def plane(i, carry):
                bonds_of(edge + planes + 1 + i, high_far[0, i], high_far[1, i], high_far[2, i], high_far[2, i - 1])
                return carry

            lax.fori_loop(1, depth - 2, plane, 0)

        pl.when(far_below)(below)
        pl.when(far_above)(above)

    def half_sweep(r, colour, parts):
        other = 1 - colour

        def turned(p):
            east, west, after, before, upper, lower = [bonds[p, colour, i] for i in range(6)]
            field, spin = [], []
            for k in range(comps):
                q = work[r, other, p, k]
                north = jnp.where(row == half - 1, q, pltpu.roll(q, half - 1, 0))
                south = jnp.where(row == 0, q, pltpu.roll(q, 1, 0))
                h = east * pltpu.roll(q, cols - 1, 1) + west * pltpu.roll(q, 1, 1)
                h = h + after * north + before * south
                h = h + upper * work[r, other, p + 1, k] + lower * work[r, other, p - 1, k]
                field.append(h)
                spin.append(work[r, colour, p, k])
            along = sum(s * h for s, h in zip(spin, field))
            strength = sum(h * h for h in field)
            scale = 2.0 * along / jnp.maximum(strength, 1.0)
            return [scale * h - s for s, h in zip(spin, field)]

        planes_of = list(parts)
        new = [turned(p) for p in planes_of]
        for p, value in zip(planes_of, new):
            for k in range(comps):
                work[r, colour, p, k] = value[k]

    low_edge, top = edge, edge + planes - 1

    def sweep_range(r, colour, first, last):
        count = last - first
        step = max(g for g in range(1, GROUP + 1) if count % g == 0)

        def some_planes(i, carry):
            half_sweep(r, colour, [first + i * step + n for n in range(step)])
            return carry

        lax.fori_loop(0, count // step, some_planes, 0)

    def inner(r):
        sweep_range(r, 0, low_edge + 1, top)
        sweep_range(r, 1, low_edge + 2, top - 1)

    def outer(r, side):
        half_sweep(r, 0, ([low_edge - 1, low_edge], [top, top + 1])[side])
        half_sweep(r, 1, ([low_edge, low_edge + 1], [top - 1, top])[side])

    def advance(r, e):
        for side in (1, 0):
            if skips(r, e):
                take_far(r, e - 1, side)
            take_halo(r, e, side)
            outer(r, side)
            if e < rounds - 1:
                send_halo(r, e + 1, (1 - side,))
                if deepens(r, e + 1):
                    send_far(r, e + 1, (1 - side,))
            elif 1 <= r < pairs:
                for n in range(len(remote)):
                    for i in ((0, 2), (1, 3))[side]:
                        result_copy(n, r, i).start()

    def prepare(r, e):
        inner(r)
        if e == rounds - 1 and 1 <= r < pairs:
            for n in range(len(remote)):
                for i in kept_back:
                    result_copy(n, r, i).start()

    def settle(n, parts):
        for i in parts:
            raw_copy(n, i).wait_recv()
        for i in parts:
            c, start, count = pieces[i]
            for p in range(start, start + count):
                for k in range(comps):
                    work[pairs + n, c, p + edge, k] = raw[pairs + n, c, p, k]

    own = list(range(pairs - 1, -1, -1))
    send_halo(own[0], 0)
    for copy in bond_copies:
        copy.start()
    for n in range(len(remote)):
        for i in sent:
            raw_copy(n, i).start()
    if far:
        for side, copy in far_bonds:
            pl.when((far_above, far_below)[side])(copy.start)
    for n in range(len(remote)):
        for i in kept_back:
            raw_copy(n, i).start()
    lax.fori_loop(1, planes, own_bonds, 0)
    for r in own[1:]:
        send_halo(r, 0)
    for r in own:
        inner(r)
    for copy in bond_copies:
        copy.wait()
    bonds_of(edge - 1, low[0, 1], low[1, 1], low[2, 1], low[2, 0])
    bonds_of(edge, coup[0, 0], coup[1, 0], coup[2, 0], low[2, 1])
    bonds_of(edge + planes, high[0], high[1], high[2], coup[2, planes - 1])

    advance(own[0], 0)
    for n, g in enumerate(guests):
        settle(n, sent)
        send_halo(g, 0)
    for r in own[1:]:
        advance(r, 0)
    for r in own:
        prepare(r, 1)
    if far:
        take_far_bonds()

    advance(own[0], 1)
    prepare(own[0], 2)
    for n, g in enumerate(guests):
        settle(n, kept_back)
    for g in guests:
        inner(g)
        advance(g, 0)
        prepare(g, 1)
    for r in own[1:]:
        advance(r, 1)
        prepare(r, 2)
    for e in range(2, rounds):
        for r in own[:1] + guests + own[1:]:
            late = e - 1 if r in guests else e
            advance(r, late)
            if late < rounds - 1:
                prepare(r, late + 1)

    def write(j, count, place):
        if j in remote:
            n = remote.index(j)
            given = lambda r, p, c, k: res[n, r - 1, c, p, k] if r else work[pairs + n, c, p + edge, k]
        else:
            given = lambda r, p, c, k: work[r, c, p + edge, k]

        def write_plane(i, carry):
            p = place(i)
            mask = front(p + edge)
            for slot in (2 * j, 2 * j + 1):
                pair = lax.rem(source[group * rep_dev + slot], rep_dev) // 2
                for k in range(comps):
                    colours = []
                    for c in range(2):
                        value = given(0, p, c, k)
                        for r in range(1, pairs):
                            value = jnp.where(pair == r, given(r, p, c, k), value)
                        colours.append(jnp.where(kept[slot], work[j, c, p + edge, k], value))
                    zero, one = colours
                    out[slot, k, p, :half] = jnp.where(mask, zero, one)
                    out[slot, k, p, half:] = reverse_rows(jnp.where(mask, one, zero), row)
            return carry

        lax.fori_loop(0, count, write_plane, 0)

    middle = (planes - 2 * WIDTH, lambda i: i + WIDTH)
    outside = (2 * WIDTH, lambda i: i + i // WIDTH * (planes - 2 * WIDTH))
    for j in range(pairs):
        if j not in remote:
            write(j, planes, lambda i: i)
    for n in range(len(remote)):
        for r in range(1, pairs):
            for i in kept_back:
                result_copy(n, r, i).wait_recv()
    for j in remote:
        write(j, *middle)
    for g in guests:
        advance(g, rounds - 1)
    for n in range(len(remote)):
        for i in range(len(pieces)):
            raw_copy(n, i).wait_send()
        for r in range(1, pairs):
            for i in kept_back:
                result_copy(n, r, i).wait_send()
            for i in sent:
                result_copy(n, r, i).wait()
    for j in remote:
        write(j, *outside)


def solution(mesh):
    n_rep, n_slab = mesh.shape["rep"], mesh.shape["slab"]

    def local(spins, couplings, source):
        rep_dev, comps, planes, rows, cols = spins.shape
        pairs, half = rep_dev // 2, rows // 2
        n_remote = sum(1 for j in range(pairs) if (1 + j) % n_rep)
        depth = min(FAR, planes)
        spare = max(depth - WIDTH, 1)
        deep = planes + 2 * depth
        starts = pairs + n_remote
        f32, i32, dma = jnp.float32, jnp.int32, pltpu.SemaphoreType.DMA
        return pl.pallas_call(
            functools.partial(kernel, n_rep, n_slab),
            out_shape=pltpu.VMEM(spins.shape, f32),
            in_specs=[
                pl.BlockSpec(memory_space=pltpu.SMEM),
                pl.BlockSpec(memory_space=pl.ANY),
                pl.BlockSpec(memory_space=pl.ANY),
            ],
            out_specs=pl.BlockSpec(memory_space=pltpu.VMEM),
            scratch_shapes=[
                pltpu.VMEM(spins.shape, f32),
                pltpu.VMEM(couplings.shape, i32),
                pltpu.VMEM((starts, 2, planes, comps, half, cols), f32),
                pltpu.VMEM((starts, 2, deep, comps, half, cols), f32),
                pltpu.VMEM((deep, 2, 6, half, cols), f32),
                pltpu.VMEM((3, WIDTH, rows, cols), i32),
                pltpu.VMEM((3, rows, cols), i32),
                pltpu.VMEM((3, spare + 1, rows, cols), i32),
                pltpu.VMEM((3, spare, rows, cols), i32),
                pltpu.VMEM((max(n_remote, 1), pairs - 1, 2, planes, comps, half, cols), f32),
                pltpu.VMEM((starts, SWEEPS, 2, WIDTH + 1, comps, half, cols), f32),
                pltpu.VMEM((starts, (SWEEPS + 1) // 2, 2, 2, spare, comps, half, cols), f32),
                pltpu.VMEM((starts, max((SWEEPS - 1) // 2, 1), 2, 2, spare, comps, half, cols), f32),
                dma((6,)),
                dma((6,)),
                dma((starts, SWEEPS, 2, 2)),
                dma((starts, SWEEPS, 2, 2)),
                dma((starts, (SWEEPS + 1) // 2, 2, 2)),
                dma((starts, (SWEEPS + 1) // 2, 2, 2)),
                dma((max(n_remote, 1), 6)),
                dma((max(n_remote, 1), 6)),
                dma((max(n_remote, 1), pairs - 1, 6)),
                dma((max(n_remote, 1), pairs - 1, 6)),
                dma((pairs + 1,)),
            ],
            compiler_params=pltpu.CompilerParams(collective_id=0, has_side_effects=True),
        )(source, spins, couplings)

    in_specs = (P("rep", None, "slab", None, None), P(None, "slab", None, None), P())
    out_specs = P("rep", None, "slab", None, None)
    return jax.shard_map(local, mesh=mesh, in_specs=in_specs, out_specs=out_specs, check_vma=False)
```
